32 devices in a mesh: gx: 8 (over z, core), gy: 4 (over y, x).
Axes of the slice: x: 2, y: 2, z: 4, core: 2. Of those that a mesh axis runs over, the one named last changes fastest.
Arguments:
- features: bfloat16 [32, 64, 32, 128], P(None, 'gx', 'gy'), may hold values from -6 to 6
- occupancy: int32 [8, 4, 16], replicated, may hold values 0 or 1
- weight_one: bfloat16 [32, 3, 3, 3, 32], replicated, may hold values from -0.21875 to 0.21875
- bias_one: float32 [32], replicated, may hold values from -3 to 3
- weight_two: bfloat16 [32, 3, 3, 3, 32], replicated, may hold values from -0.21875 to 0.21875
- bias_two: float32 [32], replicated, may hold values from -3 to 3
- grad_pooled: bfloat16 [32, 32, 16, 64], P(None, 'gx', 'gy'), may hold values from -24 to 24
- pool_choice: int32 [32, 32, 16, 64], P(None, 'gx', 'gy'), may hold values from 0 to 7
Outputs:
- grad_input: bfloat16 [32, 64, 32, 128], P(None, 'gx', 'gy')
- grad_weight_one: float32 [32, 3, 3, 3, 32], replicated
- grad_bias_one: float32 [32], replicated
- grad_weight_two: float32 [32, 3, 3, 3, 32], replicated
- grad_bias_two: float32 [32], replicated
The draws below stay inside these ranges and needn't reach their ends.
All inputs are finite; a program needn't handle non-finite values.
Results may differ from the reference program's by a relative error of at most 0.035.
The reference program's roundings to bfloat16 on the way (of `masked`, `hidden`, `upstream`, `delta_two` and `delta_one`) count: a program that leaves them out, or rounds other values in their place, can miss the bound.
Values may be sent and summed in bfloat16 or wider, within the bound.
A program may use at most 64 MiB of HBM per device.

```python
import math
import jax
import jax.numpy as jnp
from jax import lax

C = 32
NX = 64
NY = 32
NZ = 128


def touch_ends(array, stream_key, least, high):
    place = [jax.random.randint(jax.random.fold_in(stream_key, axis), (), 0, length) for axis, length in enumerate(array.shape)]
    longest = array.shape.index(max(array.shape))
    next_to = place[:longest] + [(place[longest] + 1) % array.shape[longest]] + place[longest + 1:]
    return array.at[tuple(place)].set(least).at[tuple(next_to)].set(high)


def shard_levels(key, extent, shards, least, top_value):
    def one(dim, blocks):
        heights = jax.random.uniform(jax.random.fold_in(jax.random.fold_in(key, 6), dim), (blocks,), jnp.float32, least / len(shards), top_value / len(shards))
        return jnp.repeat(jnp.exp(heights), extent[dim] // blocks).reshape((-1,) + (1,) * (len(extent) - dim - 1))

    gain = one(*shards[0])
    for cut in shards[1:]:
        gain = gain * one(*cut)
    return gain


def noise(own_key, extent, scale, most, split=(), held_as=jnp.bfloat16):
    drawn = scale * jax.random.normal(own_key, extent, jnp.float32)
    if split:
        drawn = drawn * shard_levels(own_key, extent, split, -0.22, 0.18)
    return jnp.clip(drawn, -most, most).astype(held_as)


def setup_inputs(seed: int = 0) -> dict:
    key_of = jax.random.split(jax.random.key(seed), 9)
    return {
        "features": noise(key_of[0], (C, NX, NY, NZ), 1.0, 6.0, ((1, 8), (2, 4))),
        "occupancy": touch_ends((jax.random.randint(key_of[1], (NX // 8, NY // 8, NZ // 8), 0, 4) < 3).astype(jnp.int32), jax.random.fold_in(key_of[1], 1), 0, 1),
        "weight_one": noise(key_of[2], (C, 3, 3, 3, C), (27 * C) ** -0.5, 0.21875),
        "bias_one": noise(key_of[3], (C,), 0.5, 3.0, (), jnp.float32),
        "weight_two": noise(key_of[4], (C, 3, 3, 3, C), (27 * C) ** -0.5, 0.21875),
        "bias_two": noise(key_of[5], (C,), 0.5, 3.0, (), jnp.float32),
        "grad_pooled": noise(key_of[6], (C, NX // 2, NY // 2, NZ // 2), 4.0, 24.0, ((1, 8), (2, 4))),
        "pool_choice": touch_ends(jax.random.randint(key_of[7], (C, NX // 2, NY // 2, NZ // 2), 0, 8), jax.random.fold_in(key_of[7], 1), 0, 7).astype(jnp.int32),
    }


def convolve(inputs, weight):
    kernel = weight.transpose(0, 4, 1, 2, 3)
    result = lax.conv_general_dilated(inputs[None], kernel, (1, 1, 1), [(1, 1), (1, 1), (1, 1)], dimension_numbers=('NCDHW', 'OIDHW', 'NCDHW'), precision=lax.Precision.HIGHEST)
    return result[0]

def expand(field, factor):
    return jnp.repeat(jnp.repeat(jnp.repeat(field, factor, axis=-3), factor, axis=-2), factor, axis=-1)

def reference(features, occupancy, weight_one, bias_one, weight_two, bias_two, grad_pooled, pool_choice):
    mask = expand(occupancy, 8).astype(jnp.float32)
    masked = features.astype(jnp.float32) * mask
    first_f = weight_one.astype(jnp.float32)
    second_f = weight_two.astype(jnp.float32)
    conv_one, pull_one = jax.vjp(convolve, masked, first_f)
    pre_one = conv_one + bias_one[:, None, None, None]
    hidden = (jnp.maximum(pre_one, 0.0) * mask).astype(jnp.bfloat16)
    conv_two, pull_two = jax.vjp(convolve, hidden.astype(jnp.float32), second_f)
    pre_two = conv_two + bias_two[:, None, None, None]
    spread = expand(grad_pooled.astype(jnp.float32), 2)
    chosen = expand(pool_choice, 2)
    xpos = jnp.arange(NX, dtype=jnp.int32)[:, None, None] % 2
    ypos = jnp.arange(NY, dtype=jnp.int32)[None, :, None] % 2
    zpos = jnp.arange(NZ, dtype=jnp.int32)[None, None, :] % 2
    code = 4 * xpos + 2 * ypos + zpos
    upstream = jnp.where(chosen == code[None], spread, 0.0)
    delta_two = (upstream * (pre_two > 0).astype(jnp.float32) * mask).astype(jnp.bfloat16)
    back_one, grad_w_two = pull_two(delta_two.astype(jnp.float32))
    delta_one = (back_one * (pre_one > 0).astype(jnp.float32) * mask).astype(jnp.bfloat16)
    back_input, grad_w_one = pull_one(delta_one.astype(jnp.float32))
    scale = 1.0 / math.sqrt(NX * NY * NZ)
    grad_input = (back_input * mask).astype(jnp.bfloat16)
    grad_b_one = lax.optimization_barrier(jnp.sum(delta_one.astype(jnp.float32), axis=(1, 2, 3))) * scale
    grad_b_two = lax.optimization_barrier(jnp.sum(delta_two.astype(jnp.float32), axis=(1, 2, 3))) * scale
    return (grad_input, grad_w_one * scale, grad_b_one, grad_w_two * scale, grad_b_two)
```

```python
import functools
import math

import jax
import jax.numpy as jnp
import numpy as np
from jax import lax
from jax.experimental import pallas as pl
from jax.experimental.pallas import tpu as pltpu
from jax.sharding import PartitionSpec as P

MESH = pl.DeviceIdType.MESH
HALO = 4
SIDES = tuple((sx, sy) for sx in (-1, 0, 1) for sy in (-1, 0, 1) if (sx, sy) != (0, 0))
BF = jnp.bfloat16
F32 = jnp.float32


def edge(side, cells, width):
    if side == 0:
        return 0, cells
    return (0, width) if side < 0 else (cells - width, width)


def landing(side, cells, width):
    if side == 0:
        return width, cells
    return (width + cells, width) if side < 0 else (0, width)


def exchange_kernel(nx, ny, depth, own_f, own_p, out_f, out_p, send_sem, recv_sem, local_sem):
    gx = lax.axis_index("gx")
    gy = lax.axis_index("gy")
    pairs = ((own_f, out_f, HALO), (own_p, out_p, 1))

    def exists(sx, sy):
        ok_x = jnp.logical_and(gx + sx >= 0, gx + sx < nx)
        ok_y = jnp.logical_and(gy + sy >= 0, gy + sy < ny)
        return jnp.logical_and(ok_x, ok_y)

    barrier = pltpu.get_barrier_semaphore()
    for sx, sy in SIDES:
        @pl.when(exists(sx, sy))
        def _():
            pl.semaphore_signal(barrier, inc=1, device_id=(gx + sx, gy + sy), device_id_type=MESH)
    locals_ = []
    for n, (own, out, width) in enumerate(pairs):
        cx, cy = own.shape[0], own.shape[2] // depth
        locals_.append(
            pltpu.make_async_copy(
                own, out.at[width : width + cx, :, width * depth : (width + cy) * depth], local_sem.at[n]
            )
        )
    for copy in locals_:
        copy.start()
    span_x = 1 + (gx > 0).astype(jnp.int32) + (gx < nx - 1).astype(jnp.int32)
    span_y = 1 + (gy > 0).astype(jnp.int32) + (gy < ny - 1).astype(jnp.int32)
    pl.semaphore_wait(barrier, span_x * span_y - 1)

    def copy_of(n, k):
        own, out, width = pairs[n]
        sx, sy = SIDES[k]
        cx, cy = own.shape[0], own.shape[2] // depth
        fx, lx = edge(sx, cx, width)
        fy, ly = edge(sy, cy, width)
        tx, _ = landing(sx, cx, width)
        ty, _ = landing(sy, cy, width)
        return pltpu.make_async_remote_copy(
            src_ref=own.at[fx : fx + lx, :, fy * depth : (fy + ly) * depth],
            dst_ref=out.at[tx : tx + lx, :, ty * depth : (ty + ly) * depth],
            send_sem=send_sem.at[n, k],
            recv_sem=recv_sem.at[n, k],
            device_id=(gx + sx, gy + sy),
            device_id_type=MESH,
        )

    for k, (sx, sy) in enumerate(SIDES):
        @pl.when(exists(sx, sy))
        def _():
            for n in range(2):
                copy_of(n, k).start()
    for copy in locals_:
        copy.wait()
    for k, (sx, sy) in enumerate(SIDES):
        @pl.when(exists(sx, sy))
        def _():
            for n in range(2):
                copy_of(n, k).wait_send()

        @pl.when(exists(-sx, -sy))
        def _():
            for n in range(2):
                copy_of(n, k).wait_recv()


def compute_kernel(
    cx, cy, depth, chans,
    f_ref, p_ref, mz_ref, w1_ref, w2_ref, w2b_ref, w1b_ref, b1_ref, b2_ref,
    gin_ref, gw_ref, s1, s2, s3, s4, bias_acc,
):
    lane = lax.broadcasted_iota(jnp.int32, (1, depth), 1)
    not_first = lane != 0
    not_last = lane != depth - 1
    lane_odd = lane % 2

    def mask_row(x, first, count):
        bx = (x + 8 - HALO) // 8
        flags = mz_ref[bx]
        parts = []
        for y in range(first, first + count):
            by = (y + 8 - HALO) // 8
            parts.append(flags[by : by + 1, :])
        return jnp.concatenate(parts, axis=1)

    def put(stack, x, value):
        count = value.shape[1] // depth
        rounded = value.astype(BF)
        wide = rounded.astype(F32)
        before, after = [], []
        for y in range(count):
            tile = wide[:, y * depth : (y + 1) * depth]
            before.append(jnp.where(not_first, pltpu.roll(tile, 1, 1), 0.0))
            after.append(jnp.where(not_last, pltpu.roll(tile, depth - 1, 1), 0.0))
        stack[x, 0:chans, :] = jnp.concatenate(before, axis=1).astype(BF)
        stack[x, chans : 2 * chans, :] = rounded
        stack[x, 2 * chans : 3 * chans, :] = jnp.concatenate(after, axis=1).astype(BF)

    def conv(weight, stack, x):
        width = stack.shape[2]
        rows = stack[pl.ds(x, 3)].reshape(9 * chans, width)
        full = jnp.dot(weight[...], rows, preferred_element_type=F32)
        keep = width - 2 * depth
        total = full[0:chans, 0:keep]
        total += full[chans : 2 * chans, depth : depth + keep]
        total += full[2 * chans : 3 * chans, 2 * depth : 2 * depth + keep]
        return total

    def grad(slot, delta, stack, x, first):
        width = (cy + 2) * depth
        rows = stack[pl.ds(x, 3), :, first * depth : first * depth + width].reshape(9 * chans, width)
        shifted = []
        for b in range(3):
            parts = []
            if b:
                parts.append(jnp.zeros((chans, b * depth), BF))
            parts.append(delta)
            if b < 2:
                parts.append(jnp.zeros((chans, (2 - b) * depth), BF))
            shifted.append(jnp.concatenate(parts, axis=1))
        left = jnp.concatenate(shifted, axis=0)
        gw_ref[slot, :, 0 : 9 * chans] += lax.dot_general(
            left, rows, (((1,), (1,)), ((), ())), preferred_element_type=F32
        )
        bias_acc[slot] += delta.astype(F32)

    gw_ref[...] = jnp.zeros_like(gw_ref)
    bias_acc[...] = jnp.zeros_like(bias_acc)

    @pl.loop(0, cx + 8)
    def _(x):
        mask = mask_row(x, 0, cy + 8)
        put(s1, x, jnp.where(mask > 0, f_ref[x].astype(F32), 0.0))

    @pl.loop(0, cx + 6)
    def _(x):
        mask = mask_row(x + 1, 1, cy + 6)
        pre = conv(w1_ref, s1, x) + b1_ref[...]
        put(s2, x, jnp.where(mask > 0, jnp.maximum(pre, 0.0), 0.0))

    @pl.loop(0, cx + 4)
    def _(x):
        mask = mask_row(x + 2, 2, cy + 4)
        pre = conv(w2_ref, s2, x) + b2_ref[...]
        pooled = p_ref[x // 2].astype(F32)
        vals, hits = [], []
        for y in range(cy + 4):
            half = y // 2
            code = (4 * (x % 2) + 2 * (y % 2) + lane_odd).astype(F32)
            vals.append(pooled[0:chans, half * depth : (half + 1) * depth])
            hits.append(
                jnp.where(pooled[chans : 2 * chans, half * depth : (half + 1) * depth] == code, 1.0, 0.0)
            )
        up = jnp.concatenate(vals, axis=1)
        hit = jnp.concatenate(hits, axis=1) * mask
        chosen = jnp.where(pre > 0, hit, 0.0)
        put(s3, x, jnp.where(chosen > 0, up, 0.0))

    @pl.loop(0, cx)
    def _(x):
        delta = s3[x + 2, chans : 2 * chans, 2 * depth : (2 + cy) * depth]
        grad(1, delta, s2, x + 2, 2)

    @pl.loop(0, cx + 2)
    def _(x):
        back = conv(w2b_ref, s3, x)
        hidden = s2[x + 2, chans : 2 * chans, 2 * depth : (4 + cy) * depth].astype(F32)
        put(s4, x, jnp.where(hidden > 0, back, 0.0))

    @pl.loop(0, cx)
    def _(x):
        delta = s4[x + 1, chans : 2 * chans, depth : (1 + cy) * depth]
        grad(0, delta, s1, x + 3, 3)

    @pl.loop(0, cx)
    def _(x):
        mask = mask_row(x + 4, 4, cy)
        back = conv(w1b_ref, s4, x)
        gin_ref[x] = jnp.where(mask > 0, back, 0.0).astype(BF)

    for slot in range(2):
        total = jnp.sum(bias_acc[slot], axis=1, keepdims=True)
        gw_ref[slot, 0:chans, 9 * chans :] = jnp.broadcast_to(
            total, (chans, gw_ref.shape[2] - 9 * chans)
        )


def sum_kernel(nx, ny, g_ref, o_ref, r1, h, r2, s1, q1, s2, q2, s3, q3, s4, q4):
    gx = lax.axis_index("gx")
    gy = lax.axis_index("gy")

    def peer_x(k):
        return lax.rem(gx + k, nx)

    def peer_y(k):
        return lax.rem(gy + k, ny)

    barrier = pltpu.get_barrier_semaphore()
    for k in range(1, ny):
        pl.semaphore_signal(barrier, inc=1, device_id=(gx, peer_y(k)), device_id_type=MESH)
    for k in range(1, nx):
        pl.semaphore_signal(barrier, inc=1, device_id=(peer_x(k), gy), device_id_type=MESH)
    pl.semaphore_wait(barrier, nx + ny - 2)

    def remote(src, dst, ss, rs, k, device):
        return pltpu.make_async_remote_copy(
            src_ref=src, dst_ref=dst, send_sem=ss.at[k], recv_sem=rs.at[k],
            device_id=device, device_id_type=MESH,
        )

    def run(copies):
        for c in copies:
            c.start()
        for c in copies:
            c.wait_send()
        for c in copies:
            c.wait_recv()

    run([remote(g_ref.at[peer_y(k)], r1.at[k], s1, q1, k, (gx, peer_y(k))) for k in range(1, ny)])
    part = g_ref[gy].astype(F32)
    for k in range(1, ny):
        part += r1[k].astype(F32)
    h[...] = part.astype(BF)
    run([remote(h.at[peer_x(k)], r2.at[k], s2, q2, k, (peer_x(k), gy)) for k in range(1, nx)])
    full = h[gx].astype(F32)
    for k in range(1, nx):
        full += r2[k].astype(F32)
    o_ref[gy, gx] = full.astype(BF)
    run([
        remote(o_ref.at[gy, gx], o_ref.at[gy, gx], s3, q3, k, (peer_x(k), gy)) for k in range(1, nx)
    ])
    run([remote(o_ref.at[gy], o_ref.at[gy], s4, q4, k, (gx, peer_y(k))) for k in range(1, ny)])


def rows_of(weight):
    channels = weight.shape[0]
    return weight.transpose(2, 0, 1, 3, 4).reshape(3 * channels, -1)


def flipped(weight):
    return jnp.flip(weight, (1, 2, 3)).transpose(4, 1, 2, 3, 0)


def vmem(count):
    return [pl.BlockSpec(memory_space=pltpu.VMEM)] * count


def body(features, occupancy, weight_one, bias_one, weight_two, bias_two, grad_pooled, pool_choice):
    chans, cx, cy, depth = features.shape
    nx, ny = lax.axis_size("gx"), lax.axis_size("gy")
    brick_x, brick_y = cx // 8, cy // 8
    padded_flags = jnp.pad(occupancy, ((1, 1), (1, 1), (0, 0)))
    flags = lax.dynamic_slice(
        padded_flags,
        (lax.axis_index("gx") * brick_x, lax.axis_index("gy") * brick_y, jnp.int32(0)),
        (brick_x + 2, brick_y + 2, occupancy.shape[2]),
    )
    mz = jnp.repeat(flags, 8, axis=2).astype(F32)
    own_f = features.transpose(1, 0, 2, 3).reshape(cx, chans, cy * depth)
    spread = np.repeat(np.eye(depth // 2, dtype=np.float32), 2, axis=1)
    both = jnp.concatenate([grad_pooled, pool_choice.astype(BF)], axis=0)
    both = both.transpose(1, 0, 2, 3)
    both = jnp.dot(both, jnp.asarray(spread, BF), preferred_element_type=F32).astype(BF)
    own_p = both.reshape(cx // 2, 2 * chans, (cy // 2) * depth)

    shapes = (
        jax.ShapeDtypeStruct((cx + 2 * HALO, chans, (cy + 2 * HALO) * depth), BF),
        jax.ShapeDtypeStruct((cx // 2 + 2, 2 * chans, (cy // 2 + 2) * depth), BF),
    )
    wide_f, wide_p = pl.pallas_call(
        functools.partial(exchange_kernel, nx, ny, depth),
        out_shape=shapes,
        in_specs=vmem(2),
        out_specs=tuple(vmem(2)),
        scratch_shapes=[
            pltpu.SemaphoreType.DMA((2, 8)),
            pltpu.SemaphoreType.DMA((2, 8)),
            pltpu.SemaphoreType.DMA((2,)),
        ],
        compiler_params=pltpu.CompilerParams(collective_id=0, has_side_effects=True),
        name="exchange",
    )(own_f, own_p)

    lanes = -(-(9 * chans + 1) // 128) * 128
    gin, gw = pl.pallas_call(
        functools.partial(compute_kernel, cx, cy, depth, chans),
        out_shape=(
            jax.ShapeDtypeStruct((cx, chans, cy * depth), BF),
            jax.ShapeDtypeStruct((2, 3 * chans, lanes), F32),
        ),
        in_specs=vmem(9),
        out_specs=tuple(vmem(2)),
        scratch_shapes=[
            pltpu.VMEM((cx + 8, 3 * chans, (cy + 8) * depth), BF),
            pltpu.VMEM((cx + 6, 3 * chans, (cy + 6) * depth), BF),
            pltpu.VMEM((cx + 4, 3 * chans, (cy + 4) * depth), BF),
            pltpu.VMEM((cx + 2, 3 * chans, (cy + 2) * depth), BF),
            pltpu.VMEM((2, chans, cy * depth), F32),
        ],
        compiler_params=pltpu.CompilerParams(vmem_limit_bytes=48 * 2**20),
        name="compute",
    )(
        wide_f, wide_p, mz,
        rows_of(weight_one), rows_of(weight_two),
        rows_of(flipped(weight_two)), rows_of(flipped(weight_one)),
        bias_one[:, None], bias_two[:, None],
    )

    rows = 6 * chans
    each = -(-rows // (nx * ny))
    flat = gw.reshape(rows, lanes).astype(BF)
    flat = jnp.pad(flat, ((0, each * nx * ny - rows), (0, 0)))
    summed = pl.pallas_call(
        functools.partial(sum_kernel, nx, ny),
        out_shape=jax.ShapeDtypeStruct((ny, nx, each, lanes), BF),
        in_specs=vmem(1),
        out_specs=vmem(1)[0],
        scratch_shapes=[
            pltpu.VMEM((ny, nx, each, lanes), BF),
            pltpu.VMEM((nx, each, lanes), BF),
            pltpu.VMEM((nx, each, lanes), BF),
        ]
        + [pltpu.SemaphoreType.DMA((n,)) for n in (ny, ny, nx, nx, nx, nx, ny, ny)],
        compiler_params=pltpu.CompilerParams(collective_id=1, has_side_effects=True),
        name="total",
    )(flat.reshape(ny, nx, each, lanes))
    total_cells = cx * nx * cy * ny * depth
    scale = 1.0 / math.sqrt(total_cells)
    sums = summed.reshape(-1, lanes)[:rows].astype(F32) * scale
    sums = sums.reshape(2, 3 * chans, lanes)
    grads = sums[:, :, : 9 * chans].reshape(2, 3, chans, 3, 3, chans).transpose(0, 2, 3, 1, 4, 5)
    biases = sums[:, :chans, 9 * chans]
    grad_input = gin.reshape(cx, chans, cy, depth).transpose(1, 0, 2, 3)
    return grad_input, grads[0], biases[0], grads[1], biases[1]


def solution(mesh):
    placed = (
        P(None, "gx", "gy", None),
        P(),
        P(),
        P(),
        P(),
        P(),
        P(None, "gx", "gy", None),
        P(None, "gx", "gy", None),
    )
    return jax.shard_map(
        body,
        mesh=mesh,
        in_specs=placed,
        out_specs=(P(None, "gx", "gy", None), P(), P(), P(), P()),
        check_vma=False,
    )
```

```python
import functools
import math

import jax
import jax.numpy as jnp
import numpy as np
from jax import lax
from jax.experimental import pallas as pl
from jax.experimental.pallas import tpu as pltpu
from jax.sharding import PartitionSpec as P

MESH = pl.DeviceIdType.MESH
HALO = 2
SIDES = tuple((sx, sy) for sx in (-1, 0, 1) for sy in (-1, 0, 1) if (sx, sy) != (0, 0))
BF = jnp.bfloat16
F32 = jnp.float32


def edge(side, cells):
    if side == 0:
        return 0, cells
    return (0, HALO) if side < 0 else (cells - HALO, HALO)


def landing(side, cells):
    if side == 0:
        return HALO
    return HALO + cells if side < 0 else 0


def main_kernel(
    nx, ny, cx, cy, depth, chans,
    own_f, p_ref, mz_ref, w1_ref, w2_ref, w2b_ref, w1b_ref, b1_ref, b2_ref,
    gin_ref, gw_ref,
    wide_f, wide_d, s1, s2, s3, s4, bias_acc, send_sem, recv_sem, local_sem,
):
    gx = lax.axis_index("gx")
    gy = lax.axis_index("gy")

    def exists(sx, sy):
        ok_x = jnp.logical_and(gx + sx >= 0, gx + sx < nx)
        ok_y = jnp.logical_and(gy + sy >= 0, gy + sy < ny)
        return jnp.logical_and(ok_x, ok_y)

    barrier = pltpu.get_barrier_semaphore()
    for sx, sy in SIDES:
        @pl.when(exists(sx, sy))
        def _():
            pl.semaphore_signal(barrier, inc=1, device_id=(gx + sx, gy + sy), device_id_type=MESH)
    inner = pltpu.make_async_copy(
        own_f,
        wide_f.at[HALO : HALO + cx, :, HALO * depth : (HALO + cy) * depth],
        local_sem,
    )
    inner.start()
    span_x = 1 + (gx > 0).astype(jnp.int32) + (gx < nx - 1).astype(jnp.int32)
    span_y = 1 + (gy > 0).astype(jnp.int32) + (gy < ny - 1).astype(jnp.int32)
    pl.semaphore_wait(barrier, span_x * span_y - 1)

    def copy_of(n, k):
        sx, sy = SIDES[k]
        fx, lx = edge(sx, cx)
        fy, ly = edge(sy, cy)
        tx, ty = landing(sx, cx), landing(sy, cy)
        if n == 0:
            out = wide_f
            src = own_f.at[fx : fx + lx, :, fy * depth : (fy + ly) * depth]
        else:
            out = wide_d
            fx, fy = fx + HALO, fy + HALO
            src = wide_d.at[fx : fx + lx, :, fy * depth : (fy + ly) * depth]
        return pltpu.make_async_remote_copy(
            src_ref=src,
            dst_ref=out.at[tx : tx + lx, :, ty * depth : (ty + ly) * depth],
            send_sem=send_sem.at[n, k],
            recv_sem=recv_sem.at[n, k],
            device_id=(gx + sx, gy + sy),
            device_id_type=MESH,
        )

    def send(n):
        for k, (sx, sy) in enumerate(SIDES):
            @pl.when(exists(sx, sy))
            def _():
                copy_of(n, k).start()

    def finish(n):
        for k, (sx, sy) in enumerate(SIDES):
            @pl.when(exists(sx, sy))
            def _():
                copy_of(n, k).wait_send()

            @pl.when(exists(-sx, -sy))
            def _():
                copy_of(n, k).wait_recv()

    send(0)

    lane = lax.broadcasted_iota(jnp.int32, (1, depth), 1)
    not_first = lane != 0
    not_last = lane != depth - 1
    lane_odd = lane % 2

    def mask_row(x, first, count):
        flags = mz_ref[(x + 8 - HALO) // 8]
        parts = []
        for y in range(first, first + count):
            by = (y + 8 - HALO) // 8
            parts.append(flags[by : by + 1, :])
        return jnp.concatenate(parts, axis=1)

    def put(stack, x, value):
        count = value.shape[1] // depth
        rounded = value.astype(BF)
        wide = rounded.astype(F32)
        before, after = [], []
        for y in range(count):
            tile = wide[:, y * depth : (y + 1) * depth]
            before.append(jnp.where(not_first, pltpu.roll(tile, 1, 1), 0.0))
            after.append(jnp.where(not_last, pltpu.roll(tile, depth - 1, 1), 0.0))
        stack[x, 0:chans, :] = jnp.concatenate(before, axis=1).astype(BF)
        stack[x, chans : 2 * chans, :] = rounded
        stack[x, 2 * chans : 3 * chans, :] = jnp.concatenate(after, axis=1).astype(BF)

    def conv(weight, stack, x):
        width = stack.shape[2]
        rows = stack[pl.ds(x, 3)].reshape(9 * chans, width)
        full = jnp.dot(weight[...], rows, preferred_element_type=F32)
        keep = width - 2 * depth
        total = full[0:chans, 0:keep]
        total += full[chans : 2 * chans, depth : depth + keep]
        total += full[2 * chans : 3 * chans, 2 * depth : 2 * depth + keep]
        return total

    def grad(slot, delta, stack, x, first):
        width = (cy + 2) * depth
        rows = stack[pl.ds(x, 3), :, first * depth : first * depth + width].reshape(9 * chans, width)
        shifted = []
        for b in range(3):
            parts = []
            if b:
                parts.append(jnp.zeros((chans, b * depth), BF))
            parts.append(delta)
            if b < 2:
                parts.append(jnp.zeros((chans, (2 - b) * depth), BF))
            shifted.append(jnp.concatenate(parts, axis=1))
        left = jnp.concatenate(shifted, axis=0)
        gw_ref[slot, :, 0 : 9 * chans] += lax.dot_general(
            left, rows, (((1,), (1,)), ((), ())), preferred_element_type=F32
        )
        bias_acc[slot] += delta.astype(F32)

    gw_ref[...] = jnp.zeros_like(gw_ref)
    bias_acc[...] = jnp.zeros_like(bias_acc)
    inner.wait()
    finish(0)

    @pl.loop(0, cx + 4)
    def _(x):
        mask = mask_row(x, 0, cy + 4)
        put(s1, x, jnp.where(mask > 0, wide_f[x].astype(F32), 0.0))

    @pl.loop(0, cx + 2)
    def _(x):
        mask = mask_row(x + 1, 1, cy + 2)
        pre = conv(w1_ref, s1, x) + b1_ref[...]
        put(s2, x, jnp.where(mask > 0, jnp.maximum(pre, 0.0), 0.0))

    @pl.loop(0, cx)
    def _(x):
        mask = mask_row(x + 2, 2, cy)
        pre = conv(w2_ref, s2, x) + b2_ref[...]
        pooled = p_ref[x // 2].astype(F32)
        vals, hits = [], []
        for y in range(cy):
            half = y // 2
            code = (4 * (x % 2) + 2 * (y % 2) + lane_odd).astype(F32)
            vals.append(pooled[0:chans, half * depth : (half + 1) * depth])
            hits.append(
                jnp.where(pooled[chans : 2 * chans, half * depth : (half + 1) * depth] == code, 1.0, 0.0)
            )
        up = jnp.concatenate(vals, axis=1)
        hit = jnp.concatenate(hits, axis=1) * mask
        chosen = jnp.where(pre > 0, hit, 0.0)
        delta = jnp.where(chosen > 0, up, 0.0).astype(BF)
        wide_d[x + HALO, :, HALO * depth : (HALO + cy) * depth] = delta

    send(1)

    @pl.loop(0, cx)
    def _(x):
        delta = wide_d[x + HALO, :, HALO * depth : (HALO + cy) * depth]
        grad(1, delta, s2, x, 0)

    finish(1)

    @pl.loop(0, cx + 4)
    def _(x):
        mask = mask_row(x, 0, cy + 4)
        put(s3, x, jnp.where(mask > 0, wide_d[x].astype(F32), 0.0))

    @pl.loop(0, cx + 2)
    def _(x):
        back = conv(w2b_ref, s3, x)
        hidden = s2[x, chans : 2 * chans, :].astype(F32)
        put(s4, x, jnp.where(hidden > 0, back, 0.0))

    @pl.loop(0, cx)
    def _(x):
        delta = s4[x + 1, chans : 2 * chans, depth : (1 + cy) * depth]
        grad(0, delta, s1, x + 1, 1)

    @pl.loop(0, cx)
    def _(x):
        mask = mask_row(x + 2, 2, cy)
        back = conv(w1b_ref, s4, x)
        gin_ref[x] = jnp.where(mask > 0, back, 0.0).astype(BF)

    for slot in range(2):
        total = jnp.sum(bias_acc[slot], axis=1, keepdims=True)
        gw_ref[slot, 0:chans, 9 * chans :] = jnp.broadcast_to(
            total, (chans, gw_ref.shape[2] - 9 * chans)
        )


def sum_kernel(nx, ny, g_ref, o_ref, r1, h, r2, s1, q1, s2, q2, s3, q3, s4, q4):
    gx = lax.axis_index("gx")
    gy = lax.axis_index("gy")

    def peer_x(k):
        return lax.rem(gx + k, nx)

    def peer_y(k):
        return lax.rem(gy + k, ny)

    barrier = pltpu.get_barrier_semaphore()
    for k in range(1, ny):
        pl.semaphore_signal(barrier, inc=1, device_id=(gx, peer_y(k)), device_id_type=MESH)
    for k in range(1, nx):
        pl.semaphore_signal(barrier, inc=1, device_id=(peer_x(k), gy), device_id_type=MESH)
    pl.semaphore_wait(barrier, nx + ny - 2)

    def remote(src, dst, ss, rs, k, device):
        return pltpu.make_async_remote_copy(
            src_ref=src, dst_ref=dst, send_sem=ss.at[k], recv_sem=rs.at[k],
            device_id=device, device_id_type=MESH,
        )

    def run(copies):
        for c in copies:
            c.start()
        for c in copies:
            c.wait_send()
        for c in copies:
            c.wait_recv()

    run([remote(g_ref.at[peer_y(k)], r1.at[k], s1, q1, k, (gx, peer_y(k))) for k in range(1, ny)])
    part = g_ref[gy].astype(F32)
    for k in range(1, ny):
        part += r1[k].astype(F32)
    h[...] = part.astype(BF)
    run([remote(h.at[peer_x(k)], r2.at[k], s2, q2, k, (peer_x(k), gy)) for k in range(1, nx)])
    full = h[gx].astype(F32)
    for k in range(1, nx):
        full += r2[k].astype(F32)
    o_ref[gy, gx] = full.astype(BF)
    run([
        remote(o_ref.at[gy, gx], o_ref.at[gy, gx], s3, q3, k, (peer_x(k), gy)) for k in range(1, nx)
    ])
    run([remote(o_ref.at[gy], o_ref.at[gy], s4, q4, k, (gx, peer_y(k))) for k in range(1, ny)])


def rows_of(weight):
    channels = weight.shape[0]
    return weight.transpose(2, 0, 1, 3, 4).reshape(3 * channels, -1)


def flipped(weight):
    return jnp.flip(weight, (1, 2, 3)).transpose(4, 1, 2, 3, 0)


def vmem(count):
    return [pl.BlockSpec(memory_space=pltpu.VMEM)] * count


def body(features, occupancy, weight_one, bias_one, weight_two, bias_two, grad_pooled, pool_choice):
    chans, cx, cy, depth = features.shape
    nx, ny = lax.axis_size("gx"), lax.axis_size("gy")
    brick_x, brick_y = cx // 8, cy // 8
    padded_flags = jnp.pad(occupancy, ((1, 1), (1, 1), (0, 0)))
    flags = lax.dynamic_slice(
        padded_flags,
        (lax.axis_index("gx") * brick_x, lax.axis_index("gy") * brick_y, jnp.int32(0)),
        (brick_x + 2, brick_y + 2, occupancy.shape[2]),
    )
    mz = jnp.repeat(flags, 8, axis=2).astype(F32)
    own_f = features.transpose(1, 0, 2, 3).reshape(cx, chans, cy * depth)
    spread = np.repeat(np.eye(depth // 2, dtype=np.float32), 2, axis=1)
    both = jnp.concatenate([grad_pooled, pool_choice.astype(BF)], axis=0)
    both = both.transpose(1, 0, 2, 3)
    both = jnp.dot(both, jnp.asarray(spread, BF), preferred_element_type=F32).astype(BF)
    own_p = both.reshape(cx // 2, 2 * chans, (cy // 2) * depth)

    lanes = -(-(9 * chans + 1) // 128) * 128
    gin, gw = pl.pallas_call(
        functools.partial(main_kernel, nx, ny, cx, cy, depth, chans),
        out_shape=(
            jax.ShapeDtypeStruct((cx, chans, cy * depth), BF),
            jax.ShapeDtypeStruct((2, 3 * chans, lanes), F32),
        ),
        in_specs=vmem(9),
        out_specs=tuple(vmem(2)),
        scratch_shapes=[
            pltpu.VMEM((cx + 4, chans, (cy + 4) * depth), BF),
            pltpu.VMEM((cx + 4, chans, (cy + 4) * depth), BF),
            pltpu.VMEM((cx + 4, 3 * chans, (cy + 4) * depth), BF),
            pltpu.VMEM((cx + 2, 3 * chans, (cy + 2) * depth), BF),
            pltpu.VMEM((cx + 4, 3 * chans, (cy + 4) * depth), BF),
            pltpu.VMEM((cx + 2, 3 * chans, (cy + 2) * depth), BF),
            pltpu.VMEM((2, chans, cy * depth), F32),
            pltpu.SemaphoreType.DMA((2, 8)),
            pltpu.SemaphoreType.DMA((2, 8)),
            pltpu.SemaphoreType.DMA,
        ],
        compiler_params=pltpu.CompilerParams(
            collective_id=0, has_side_effects=True, vmem_limit_bytes=48 * 2**20
        ),
        name="main",
    )(
        own_f, own_p, mz,
        rows_of(weight_one), rows_of(weight_two),
        rows_of(flipped(weight_two)), rows_of(flipped(weight_one)),
        bias_one[:, None], bias_two[:, None],
    )

    rows = 6 * chans
    each = -(-rows // (nx * ny))
    flat = gw.reshape(rows, lanes).astype(BF)
    flat = jnp.pad(flat, ((0, each * nx * ny - rows), (0, 0)))
    summed = pl.pallas_call(
        functools.partial(sum_kernel, nx, ny),
        out_shape=jax.ShapeDtypeStruct((ny, nx, each, lanes), BF),
        in_specs=vmem(1),
        out_specs=vmem(1)[0],
        scratch_shapes=[
            pltpu.VMEM((ny, nx, each, lanes), BF),
            pltpu.VMEM((nx, each, lanes), BF),
            pltpu.VMEM((nx, each, lanes), BF),
        ]
        + [pltpu.SemaphoreType.DMA((n,)) for n in (ny, ny, nx, nx, nx, nx, ny, ny)],
        compiler_params=pltpu.CompilerParams(collective_id=1, has_side_effects=True),
        name="total",
    )(flat.reshape(ny, nx, each, lanes))
    total_cells = cx * nx * cy * ny * depth
    scale = 1.0 / math.sqrt(total_cells)
    sums = summed.reshape(-1, lanes)[:rows].astype(F32) * scale
    sums = sums.reshape(2, 3 * chans, lanes)
    grads = sums[:, :, : 9 * chans].reshape(2, 3, chans, 3, 3, chans).transpose(0, 2, 3, 1, 4, 5)
    biases = sums[:, :chans, 9 * chans]
    grad_input = gin.reshape(cx, chans, cy, depth).transpose(1, 0, 2, 3)
    return grad_input, grads[0], biases[0], grads[1], biases[1]


def solution(mesh):
    placed = (
        P(None, "gx", "gy", None),
        P(),
        P(),
        P(),
        P(),
        P(),
        P(None, "gx", "gy", None),
        P(None, "gx", "gy", None),
    )
    return jax.shard_map(
        body,
        mesh=mesh,
        in_specs=placed,
        out_specs=(P(None, "gx", "gy", None), P(), P(), P(), P()),
        check_vma=False,
    )
```

```python
import functools
import math

import jax
import jax.numpy as jnp
import numpy as np
from jax import lax
from jax.experimental import pallas as pl
from jax.experimental.pallas import tpu as pltpu
from jax.sharding import PartitionSpec as P

MESH = pl.DeviceIdType.MESH
HALO = 2
SIDES = tuple((sx, sy) for sx in (-1, 0, 1) for sy in (-1, 0, 1) if (sx, sy) != (0, 0))
BF = jnp.bfloat16
F32 = jnp.float32


def edge(side, cells):
    if side == 0:
        return 0, cells
    return (0, HALO) if side < 0 else (cells - HALO, HALO)


def landing(side, cells):
    if side == 0:
        return HALO
    return HALO + cells if side < 0 else 0


def main_kernel(
    nx, ny, cx, cy, depth, chans,
    own_f, p_ref, mz_ref, w1_ref, w2_ref, w2b_ref, w1b_ref, b_ref,
    gin_ref, o_ref,
    wide_f, wide_d, s1, s2, s3, s4, bias_acc, gw_ref, g_ref, r1, h, r2,
    send_sem, recv_sem, sum_send_x, sum_recv_x, sum_send_y, sum_recv_y,
):
    gx = lax.axis_index("gx")
    gy = lax.axis_index("gy")

    def exists(sx, sy):
        ok_x = jnp.logical_and(gx + sx >= 0, gx + sx < nx)
        ok_y = jnp.logical_and(gy + sy >= 0, gy + sy < ny)
        return jnp.logical_and(ok_x, ok_y)

    def peer_x(k):
        return lax.rem(gx + k, nx)

    def peer_y(k):
        return lax.rem(gy + k, ny)

    barrier = pltpu.get_barrier_semaphore()
    for k in range(1, ny):
        pl.semaphore_signal(barrier, inc=1, device_id=(gx, peer_y(k)), device_id_type=MESH)
    for k in range(1, nx):
        pl.semaphore_signal(barrier, inc=1, device_id=(peer_x(k), gy), device_id_type=MESH)
    for sx, sy in SIDES:
        if sx and sy:
            @pl.when(exists(sx, sy))
            def _():
                pl.semaphore_signal(
                    barrier, inc=1, device_id=(gx + sx, gy + sy), device_id_type=MESH
                )
    beside_x = (gx > 0).astype(jnp.int32) + (gx < nx - 1).astype(jnp.int32)
    beside_y = (gy > 0).astype(jnp.int32) + (gy < ny - 1).astype(jnp.int32)
    pl.semaphore_wait(barrier, nx + ny - 2 + beside_x * beside_y)

    def copy_of(n, k):
        sx, sy = SIDES[k]
        fx, lx = edge(sx, cx)
        fy, ly = edge(sy, cy)
        tx, ty = landing(sx, cx), landing(sy, cy)
        if n == 0:
            out = wide_f
            src = own_f.at[fx : fx + lx, fy : fy + ly]
        else:
            out = wide_d
            fx, fy = fx + HALO, fy + HALO
            src = wide_d.at[fx : fx + lx, fy : fy + ly]
        return pltpu.make_async_remote_copy(
            src_ref=src,
            dst_ref=out.at[tx : tx + lx, ty : ty + ly],
            send_sem=send_sem.at[n, k],
            recv_sem=recv_sem.at[n, k],
            device_id=(gx + sx, gy + sy),
            device_id_type=MESH,
        )

    def send(n):
        for k, (sx, sy) in enumerate(SIDES):
            @pl.when(exists(sx, sy))
            def _():
                copy_of(n, k).start()

    def finish(n):
        for k, (sx, sy) in enumerate(SIDES):
            @pl.when(exists(sx, sy))
            def _():
                copy_of(n, k).wait_send()

            @pl.when(exists(-sx, -sy))
            def _():
                copy_of(n, k).wait_recv()

    send(0)

    lane = lax.broadcasted_iota(jnp.int32, (1, depth), 1)
    not_first = lane != 0
    not_last = lane != depth - 1
    lane_odd = lane % 2

    def mask_row(x, first, count):
        flags = mz_ref[(x + 8 - HALO) // 8]
        parts = []
        for y in range(first, first + count):
            by = (y + 8 - HALO) // 8
            parts.append(flags[by : by + 1, :])
        return jnp.concatenate(parts, axis=1)

    def put(stack, x, value, first=0):
        count = value.shape[1] // depth
        rounded = value.astype(BF)
        wide = rounded.astype(F32)
        before, after = [], []
        for y in range(count):
            tile = wide[:, y * depth : (y + 1) * depth]
            before.append(jnp.where(not_first, pltpu.roll(tile, 1, 1), 0.0))
            after.append(jnp.where(not_last, pltpu.roll(tile, depth - 1, 1), 0.0))
        where = slice(first * depth, (first + count) * depth)
        stack[x, 0:chans, where] = jnp.concatenate(before, axis=1).astype(BF)
        stack[x, chans : 2 * chans, where] = rounded
        stack[x, 2 * chans : 3 * chans, where] = jnp.concatenate(after, axis=1).astype(BF)

    def tiles(ref, x, first, count):
        return jnp.concatenate([ref[x, y] for y in range(first, first + count)], axis=1)

    def put_cells(stack, ref, x, first, count):
        mask = mask_row(x, first, count)
        put(stack, x, jnp.where(mask > 0, tiles(ref, x, first, count).astype(F32), 0.0), first)

    def put_halo(stack, ref):
        @pl.loop(0, 2 * HALO)
        def _(n):
            put_cells(stack, ref, n + cx * (n // HALO), 0, cy + 2 * HALO)

        @pl.loop(HALO, HALO + cx)
        def _(x):
            put_cells(stack, ref, x, 0, HALO)
            put_cells(stack, ref, x, HALO + cy, HALO)

    def conv(weight, stack, x):
        width = stack.shape[2]
        rows = stack[pl.ds(x, 3)].reshape(9 * chans, width)
        full = jnp.dot(weight[...], rows, preferred_element_type=F32)
        keep = width - 2 * depth
        total = full[0:chans, 0:keep]
        total += full[chans : 2 * chans, depth : depth + keep]
        total += full[2 * chans : 3 * chans, 2 * depth : 2 * depth + keep]
        return total

    def grad(slot, delta, stack, x, first):
        width = (cy + 2) * depth
        rows = stack[pl.ds(x, 3), :, first * depth : first * depth + width].reshape(9 * chans, width)
        shifted = []
        for b in range(3):
            parts = []
            if b:
                parts.append(jnp.zeros((chans, b * depth), BF))
            parts.append(delta)
            if b < 2:
                parts.append(jnp.zeros((chans, (2 - b) * depth), BF))
            shifted.append(jnp.concatenate(parts, axis=1))
        left = jnp.concatenate(shifted, axis=0)
        gw_ref[slot, :, 0 : 9 * chans] += lax.dot_general(
            left, rows, (((1,), (1,)), ((), ())), preferred_element_type=F32
        )
        bias_acc[slot] += delta.astype(F32)

    each = g_ref.shape[3]

    def pack(slot):
        total = jnp.sum(bias_acc[slot], axis=1, keepdims=True)
        gw_ref[slot, 0:chans, 9 * chans :] = jnp.broadcast_to(
            total, (chans, gw_ref.shape[2] - 9 * chans)
        )
        for n in range(nx * ny):
            first = min(n * each, 3 * chans - each)
            g_ref[slot, n // nx, n % nx] = gw_ref[slot, first : first + each].astype(BF)

    def sum_copies(slot, phase):
        out = []
        along_y = phase in (0, 3)
        for k in range(1, ny if along_y else nx):
            peer = peer_y(k) if along_y else peer_x(k)
            if phase == 0:
                src, dst = g_ref.at[slot, peer], r1.at[slot, k]
            elif phase == 1:
                src, dst = h.at[slot, peer], r2.at[slot, k]
            elif phase == 2:
                src = dst = o_ref.at[slot, gy, gx]
            else:
                src = dst = o_ref.at[slot, gy]
            ss, rs = (sum_send_y, sum_recv_y) if along_y else (sum_send_x, sum_recv_x)
            out.append(pltpu.make_async_remote_copy(
                src_ref=src, dst_ref=dst,
                send_sem=ss.at[slot, phase // 2, k], recv_sem=rs.at[slot, phase // 2, k],
                device_id=(gx, peer) if along_y else (peer, gy), device_id_type=MESH,
            ))
        return out

    def sum_start(slot, phase):
        for copy in sum_copies(slot, phase):
            copy.start()

    def sum_finish(slot, phase):
        for copy in sum_copies(slot, phase):
            copy.wait_send()
            copy.wait_recv()
        if phase == 0:
            part = g_ref[slot, gy].astype(F32)
            for k in range(1, ny):
                part += r1[slot, k].astype(F32)
            h[slot] = part.astype(BF)
        if phase == 1:
            full = h[slot, gx].astype(F32)
            for k in range(1, nx):
                full += r2[slot, k].astype(F32)
            o_ref[slot, gy, gx] = full.astype(BF)

    gw_ref[...] = jnp.zeros_like(gw_ref)
    bias_acc[...] = jnp.zeros_like(bias_acc)

    @pl.loop(0, cx)
    def _(x):
        mask = mask_row(x + HALO, HALO, cy)
        put(s1, x + HALO, jnp.where(mask > 0, tiles(own_f, x, 0, cy).astype(F32), 0.0), HALO)

    finish(0)
    put_halo(s1, wide_f)

    @pl.loop(0, cx + 2)
    def _(x):
        mask = mask_row(x + 1, 1, cy + 2)
        pre = conv(w1_ref, s1, x) + b_ref[:, 0:1]
        put(s2, x, jnp.where(mask > 0, jnp.maximum(pre, 0.0), 0.0))

    @pl.loop(0, cx)
    def _(x):
        mask = mask_row(x + 2, 2, cy)
        pre = conv(w2_ref, s2, x) + b_ref[:, 1:2]
        vals, hits = [], []
        for y in range(cy):
            pooled = p_ref[x // 2, y // 2].astype(F32)
            code = (4 * (x % 2) + 2 * (y % 2) + lane_odd).astype(F32)
            vals.append(pooled[0:chans])
            hits.append(jnp.where(pooled[chans : 2 * chans] == code, 1.0, 0.0))
        up = jnp.concatenate(vals, axis=1)
        hit = jnp.concatenate(hits, axis=1) * mask
        chosen = jnp.where(pre > 0, hit, 0.0)
        delta = jnp.where(chosen > 0, up, 0.0)
        rounded = delta.astype(BF)
        for y in range(cy):
            wide_d[x + HALO, y + HALO] = rounded[:, y * depth : (y + 1) * depth]
        put(s3, x + HALO, delta, HALO)

    send(1)

    @pl.loop(0, cx)
    def _(x):
        delta = s3[x + HALO, chans : 2 * chans, HALO * depth : (HALO + cy) * depth]
        grad(1, delta, s2, x, 0)

    pack(1)
    finish(1)
    sum_start(1, 0)
    put_halo(s3, wide_d)

    @pl.loop(0, cx + 2)
    def _(x):
        back = conv(w2b_ref, s3, x)
        hidden = s2[x, chans : 2 * chans, :].astype(F32)
        put(s4, x, jnp.where(hidden > 0, back, 0.0))

    sum_finish(1, 0)
    sum_start(1, 1)

    @pl.loop(0, cx)
    def _(x):
        delta = s4[x + 1, chans : 2 * chans, depth : (1 + cy) * depth]
        grad(0, delta, s1, x + 1, 1)

    pack(0)
    sum_start(0, 0)
    sum_finish(1, 1)
    sum_start(1, 2)

    def last(x):
        mask = mask_row(x + 2, 2, cy)
        back = conv(w1b_ref, s4, x)
        out = jnp.where(mask > 0, back, 0.0).astype(BF)
        for y in range(cy):
            gin_ref[x, y] = out[:, y * depth : (y + 1) * depth]

    pl.loop(0, cx // 2)(last)
    sum_finish(0, 0)
    sum_start(0, 1)
    sum_finish(1, 2)
    sum_start(1, 3)
    pl.loop(cx // 2, cx)(last)
    sum_finish(0, 1)
    sum_start(0, 2)
    sum_finish(0, 2)
    sum_start(0, 3)
    sum_finish(1, 3)
    sum_finish(0, 3)


def rows_of(weight):
    channels = weight.shape[0]
    return weight.transpose(2, 0, 1, 3, 4).reshape(3 * channels, -1)


def flipped(weight):
    return jnp.flip(weight, (1, 2, 3)).transpose(4, 1, 2, 3, 0)


def vmem(count):
    return [pl.BlockSpec(memory_space=pltpu.VMEM)] * count


def body(features, occupancy, weight_one, bias_one, weight_two, bias_two, grad_pooled, pool_choice):
    chans, cx, cy, depth = features.shape
    nx, ny = lax.axis_size("gx"), lax.axis_size("gy")
    brick_x, brick_y = cx // 8, cy // 8
    padded_flags = jnp.pad(occupancy, ((1, 1), (1, 1), (0, 0)))
    flags = lax.dynamic_slice(
        padded_flags,
        (lax.axis_index("gx") * brick_x, lax.axis_index("gy") * brick_y, jnp.int32(0)),
        (brick_x + 2, brick_y + 2, occupancy.shape[2]),
    )
    mz = jnp.repeat(flags, 8, axis=2).astype(F32)
    own_f = features.transpose(1, 2, 0, 3)
    spread = np.repeat(np.eye(depth // 2, dtype=np.float32), 2, axis=1)
    both = jnp.concatenate([grad_pooled, pool_choice.astype(BF)], axis=0)
    both = jnp.dot(both, jnp.asarray(spread, BF), preferred_element_type=F32).astype(BF)
    own_p = both.transpose(1, 2, 0, 3)

    lanes = -(-(9 * chans + 1) // 128) * 128
    each = -(-3 * chans // (nx * ny))
    gin, summed = pl.pallas_call(
        functools.partial(main_kernel, nx, ny, cx, cy, depth, chans),
        out_shape=(
            jax.ShapeDtypeStruct((cx, cy, chans, depth), BF),
            jax.ShapeDtypeStruct((2, ny, nx, each, lanes), BF),
        ),
        in_specs=vmem(8),
        out_specs=tuple(vmem(2)),
        scratch_shapes=[
            pltpu.VMEM((cx + 4, cy + 4, chans, depth), BF),
            pltpu.VMEM((cx + 4, cy + 4, chans, depth), BF),
            pltpu.VMEM((cx + 4, 3 * chans, (cy + 4) * depth), BF),
            pltpu.VMEM((cx + 2, 3 * chans, (cy + 2) * depth), BF),
            pltpu.VMEM((cx + 4, 3 * chans, (cy + 4) * depth), BF),
            pltpu.VMEM((cx + 2, 3 * chans, (cy + 2) * depth), BF),
            pltpu.VMEM((2, chans, cy * depth), F32),
            pltpu.VMEM((2, 3 * chans, lanes), F32),
            pltpu.VMEM((2, ny, nx, each, lanes), BF),
            pltpu.VMEM((2, ny, nx, each, lanes), BF),
            pltpu.VMEM((2, nx, each, lanes), BF),
            pltpu.VMEM((2, nx, each, lanes), BF),
            pltpu.SemaphoreType.DMA((2, 8)),
            pltpu.SemaphoreType.DMA((2, 8)),
            pltpu.SemaphoreType.DMA((2, 2, nx)),
            pltpu.SemaphoreType.DMA((2, 2, nx)),
            pltpu.SemaphoreType.DMA((2, 2, ny)),
            pltpu.SemaphoreType.DMA((2, 2, ny)),
        ],
        compiler_params=pltpu.CompilerParams(
            collective_id=0, has_side_effects=True, vmem_limit_bytes=48 * 2**20
        ),
        name="main",
    )(
        own_f, own_p, mz,
        rows_of(weight_one), rows_of(weight_two),
        rows_of(flipped(weight_two)), rows_of(flipped(weight_one)),
        jnp.stack([bias_one, bias_two], axis=1),
    )

    total_cells = cx * nx * cy * ny * depth
    scale = 1.0 / math.sqrt(total_cells)
    sums = summed.astype(F32).reshape(2, -1, lanes)[:, : 3 * chans] * scale
    grads = sums[:, :, : 9 * chans].reshape(2, 3, chans, 3, 3, chans).transpose(0, 2, 3, 1, 4, 5)
    biases = sums[:, :chans, 9 * chans]
    grad_input = gin.transpose(2, 0, 1, 3)
    return grad_input, grads[0], biases[0], grads[1], biases[1]


def solution(mesh):
    placed = (
        P(None, "gx", "gy", None),
        P(),
        P(),
        P(),
        P(),
        P(),
        P(None, "gx", "gy", None),
        P(None, "gx", "gy", None),
    )
    return jax.shard_map(
        body,
        mesh=mesh,
        in_specs=placed,
        out_specs=(P(None, "gx", "gy", None), P(), P(), P(), P()),
        check_vma=False,
    )
```

```python
import functools
import math

import jax
import jax.numpy as jnp
import numpy as np
from jax import lax
from jax.experimental import pallas as pl
from jax.experimental.pallas import tpu as pltpu
from jax.sharding import PartitionSpec as P

MESH = pl.DeviceIdType.MESH
HALO = 2
SIDES = tuple((sx, sy) for sx in (-1, 0, 1) for sy in (-1, 0, 1) if (sx, sy) != (0, 0))
BF = jnp.bfloat16
F32 = jnp.float32


def edge(side, cells):
    if side == 0:
        return 0, cells
    return (0, HALO) if side < 0 else (cells - HALO, HALO)


def landing(side, cells):
    if side == 0:
        return HALO
    return HALO + cells if side < 0 else 0


def main_kernel(
    nx, ny, cx, cy, depth, chans,
    own_f, p_ref, mz_ref, w1_ref, w2_ref, w2b_ref, w1b_ref, b_ref,
    gin_ref, o_ref,
    wide_f, wide_d, s1, s2, s3, s4, bias_acc, gw_ref, g_ref, r1, h, r2,
    send_sem, recv_sem, sum_send_x, sum_recv_x, sum_send_y, sum_recv_y,
):
    gx = lax.axis_index("gx")
    gy = lax.axis_index("gy")

    def exists(sx, sy):
        ok_x = jnp.logical_and(gx + sx >= 0, gx + sx < nx)
        ok_y = jnp.logical_and(gy + sy >= 0, gy + sy < ny)
        return jnp.logical_and(ok_x, ok_y)

    def peer_x(k):
        return lax.rem(gx + k, nx)

    def peer_y(k):
        return lax.rem(gy + k, ny)

    barrier = pltpu.get_barrier_semaphore()
    for k in range(1, ny):
        pl.semaphore_signal(barrier, inc=1, device_id=(gx, peer_y(k)), device_id_type=MESH)
    for k in range(1, nx):
        pl.semaphore_signal(barrier, inc=1, device_id=(peer_x(k), gy), device_id_type=MESH)
    for sx, sy in SIDES:
        if sx and sy:
            @pl.when(exists(sx, sy))
            def _():
                pl.semaphore_signal(
                    barrier, inc=1, device_id=(gx + sx, gy + sy), device_id_type=MESH
                )
    beside_x = (gx > 0).astype(jnp.int32) + (gx < nx - 1).astype(jnp.int32)
    beside_y = (gy > 0).astype(jnp.int32) + (gy < ny - 1).astype(jnp.int32)
    pl.semaphore_wait(barrier, nx + ny - 2 + beside_x * beside_y)

    def copy_of(n, k):
        sx, sy = SIDES[k]
        fx, lx = edge(sx, cx)
        fy, ly = edge(sy, cy)
        tx, ty = landing(sx, cx), landing(sy, cy)
        if n == 0:
            out = wide_f
            src = own_f.at[fx : fx + lx, fy : fy + ly]
        else:
            out = wide_d
            fx, fy = fx + HALO, fy + HALO
            src = wide_d.at[fx : fx + lx, fy : fy + ly]
        return pltpu.make_async_remote_copy(
            src_ref=src,
            dst_ref=out.at[tx : tx + lx, ty : ty + ly],
            send_sem=send_sem.at[n, k],
            recv_sem=recv_sem.at[n, k],
            device_id=(gx + sx, gy + sy),
            device_id_type=MESH,
        )

    def send(n):
        for k, (sx, sy) in enumerate(SIDES):
            @pl.when(exists(sx, sy))
            def _():
                copy_of(n, k).start()

    def finish(n):
        for k, (sx, sy) in enumerate(SIDES):
            @pl.when(exists(sx, sy))
            def _():
                copy_of(n, k).wait_send()

            @pl.when(exists(-sx, -sy))
            def _():
                copy_of(n, k).wait_recv()

    send(0)

    same = lax.broadcasted_iota(jnp.int32, (chans, chans), 0) == lax.broadcasted_iota(
        jnp.int32, (chans, chans), 1
    )

    def column(n):
        return jnp.sum(jnp.where(same, b_ref[n : n + 1, :], 0.0), axis=1, keepdims=True)

    bias_one, bias_two = column(0), column(1)
    lane = lax.broadcasted_iota(jnp.int32, (1, depth), 1)
    not_first = lane != 0
    not_last = lane != depth - 1
    lane_odd = lane % 2

    def mask_row(x, first, count):
        brick = gx * (cx // 8) + (x + 8 - HALO) // 8
        flags = {}
        parts = []
        for y in range(first, first + count):
            by = (y + 8 - HALO) // 8
            if by not in flags:
                flags[by] = mz_ref[brick, pl.ds(gy * (cy // 8) + by, 1), :]
            parts.append(flags[by])
        return jnp.concatenate(parts, axis=1)

    def put(stack, x, value, first=0):
        count = value.shape[1] // depth
        rounded = value.astype(BF)
        wide = rounded.astype(F32)
        before, after = [], []
        for y in range(count):
            tile = wide[:, y * depth : (y + 1) * depth]
            before.append(jnp.where(not_first, pltpu.roll(tile, 1, 1), 0.0))
            after.append(jnp.where(not_last, pltpu.roll(tile, depth - 1, 1), 0.0))
        where = slice(first * depth, (first + count) * depth)
        stack[x, 0:chans, where] = jnp.concatenate(before, axis=1).astype(BF)
        stack[x, chans : 2 * chans, where] = rounded
        stack[x, 2 * chans : 3 * chans, where] = jnp.concatenate(after, axis=1).astype(BF)

    def tiles(ref, x, first, count):
        return jnp.concatenate([ref[x, y] for y in range(first, first + count)], axis=1)

    def put_cells(stack, ref, x, first, count):
        mask = mask_row(x, first, count)
        put(stack, x, jnp.where(mask > 0, tiles(ref, x, first, count).astype(F32), 0.0), first)

    def put_halo(stack, ref):
        @pl.loop(0, 2 * HALO, unroll=2)
        def _(n):
            put_cells(stack, ref, n + cx * (n // HALO), 0, cy + 2 * HALO)

        @pl.loop(HALO, HALO + cx, unroll=2)
        def _(x):
            put_cells(stack, ref, x, 0, HALO)
            put_cells(stack, ref, x, HALO + cy, HALO)

    def conv(weight, stack, x):
        width = stack.shape[2]
        rows = stack[pl.ds(x, 3)].reshape(9 * chans, width)
        full = jnp.dot(weight[...], rows, preferred_element_type=F32)
        keep = width - 2 * depth
        total = full[0:chans, 0:keep]
        total += full[chans : 2 * chans, depth : depth + keep]
        total += full[2 * chans : 3 * chans, 2 * depth : 2 * depth + keep]
        return total

    def grad(slot, delta, stack, x, first):
        width = (cy + 2) * depth
        rows = stack[pl.ds(x, 3), :, first * depth : first * depth + width].reshape(9 * chans, width)
        shifted = []
        for b in range(3):
            parts = []
            if b:
                parts.append(jnp.zeros((chans, b * depth), BF))
            parts.append(delta)
            if b < 2:
                parts.append(jnp.zeros((chans, (2 - b) * depth), BF))
            shifted.append(jnp.concatenate(parts, axis=1))
        left = jnp.concatenate(shifted, axis=0)
        gw_ref[slot, :, 0 : 9 * chans] += lax.dot_general(
            left, rows, (((1,), (1,)), ((), ())), preferred_element_type=F32
        )
        bias_acc[slot] += delta.astype(F32)

    each = g_ref.shape[3]

    def pack(slot):
        total = jnp.sum(bias_acc[slot], axis=1, keepdims=True)
        gw_ref[slot, 0:chans, 9 * chans :] = jnp.broadcast_to(
            total, (chans, gw_ref.shape[2] - 9 * chans)
        )
        for n in range(nx * ny):
            first = min(n * each, 3 * chans - each)
            g_ref[slot, n // nx, n % nx] = gw_ref[slot, first : first + each].astype(BF)

    def sum_copies(slot, phase):
        out = []
        along_y = phase in (0, 3)
        for k in range(1, ny if along_y else nx):
            peer = peer_y(k) if along_y else peer_x(k)
            if phase == 0:
                src, dst = g_ref.at[slot, peer], r1.at[slot, k]
            elif phase == 1:
                src, dst = h.at[slot, peer], r2.at[slot, k]
            elif phase == 2:
                src = dst = o_ref.at[slot, gy, gx]
            else:
                src = dst = o_ref.at[slot, gy]
            ss, rs = (sum_send_y, sum_recv_y) if along_y else (sum_send_x, sum_recv_x)
            out.append(pltpu.make_async_remote_copy(
                src_ref=src, dst_ref=dst,
                send_sem=ss.at[slot, phase // 2, k], recv_sem=rs.at[slot, phase // 2, k],
                device_id=(gx, peer) if along_y else (peer, gy), device_id_type=MESH,
            ))
        return out

    def sum_start(slot, phase):
        for copy in sum_copies(slot, phase):
            copy.start()

    def sum_finish(slot, phase):
        for copy in sum_copies(slot, phase):
            copy.wait_send()
            copy.wait_recv()
        if phase == 0:
            part = g_ref[slot, gy].astype(F32)
            for k in range(1, ny):
                part += r1[slot, k].astype(F32)
            h[slot] = part.astype(BF)
        if phase == 1:
            full = h[slot, gx].astype(F32)
            for k in range(1, nx):
                full += r2[slot, k].astype(F32)
            o_ref[slot, gy, gx] = full.astype(BF)

    gw_ref[...] = jnp.zeros_like(gw_ref)
    bias_acc[...] = jnp.zeros_like(bias_acc)

    @pl.loop(0, cx, unroll=2)
    def _(x):
        mask = mask_row(x + HALO, HALO, cy)
        put(s1, x + HALO, jnp.where(mask > 0, tiles(own_f, x, 0, cy).astype(F32), 0.0), HALO)

    finish(0)
    put_halo(s1, wide_f)

    @pl.loop(0, cx + 2, unroll=2)
    def _(x):
        mask = mask_row(x + 1, 1, cy + 2)
        pre = conv(w1_ref, s1, x) + bias_one
        put(s2, x, jnp.where(mask > 0, jnp.maximum(pre, 0.0), 0.0))

    @pl.loop(0, cx, unroll=2)
    def _(x):
        mask = mask_row(x + 2, 2, cy)
        pre = conv(w2_ref, s2, x) + bias_two
        vals, hits = [], []
        for y in range(cy):
            pooled = p_ref[x // 2, y // 2].astype(F32)
            code = (4 * (x % 2) + 2 * (y % 2) + lane_odd).astype(F32)
            vals.append(pooled[0:chans])
            hits.append(jnp.where(pooled[chans : 2 * chans] == code, 1.0, 0.0))
        up = jnp.concatenate(vals, axis=1)
        hit = jnp.concatenate(hits, axis=1) * mask
        chosen = jnp.where(pre > 0, hit, 0.0)
        delta = jnp.where(chosen > 0, up, 0.0)
        rounded = delta.astype(BF)
        for y in range(cy):
            wide_d[x + HALO, y + HALO] = rounded[:, y * depth : (y + 1) * depth]
        put(s3, x + HALO, delta, HALO)

    send(1)

    @pl.loop(0, cx, unroll=2)
    def _(x):
        delta = s3[x + HALO, chans : 2 * chans, HALO * depth : (HALO + cy) * depth]
        grad(1, delta, s2, x, 0)

    pack(1)
    finish(1)
    sum_start(1, 0)
    put_halo(s3, wide_d)

    @pl.loop(0, cx + 2, unroll=2)
    def _(x):
        back = conv(w2b_ref, s3, x)
        hidden = s2[x, chans : 2 * chans, :].astype(F32)
        put(s4, x, jnp.where(hidden > 0, back, 0.0))

    sum_finish(1, 0)
    sum_start(1, 1)

    @pl.loop(0, cx, unroll=2)
    def _(x):
        delta = s4[x + 1, chans : 2 * chans, depth : (1 + cy) * depth]
        grad(0, delta, s1, x + 1, 1)

    pack(0)
    sum_start(0, 0)
    sum_finish(1, 1)
    sum_start(1, 2)

    def last(x):
        mask = mask_row(x + 2, 2, cy)
        back = conv(w1b_ref, s4, x)
        out = jnp.where(mask > 0, back, 0.0).astype(BF)
        for y in range(cy):
            gin_ref[x, y] = out[:, y * depth : (y + 1) * depth]

    pl.loop(0, cx // 2, unroll=2)(last)
    sum_finish(0, 0)
    sum_start(0, 1)
    sum_finish(1, 2)
    sum_start(1, 3)
    pl.loop(cx // 2, cx, unroll=2)(last)
    sum_finish(0, 1)
    sum_start(0, 2)
    sum_finish(0, 2)
    sum_start(0, 3)
    sum_finish(1, 3)
    sum_finish(0, 3)


def rows_of(weight):
    channels = weight.shape[0]
    return weight.transpose(2, 0, 1, 3, 4).reshape(3 * channels, -1)


def flipped(weight):
    return jnp.flip(weight, (1, 2, 3)).transpose(4, 1, 2, 3, 0)


def vmem(count):
    return [pl.BlockSpec(memory_space=pltpu.VMEM)] * count


def body(features, occupancy, weight_one, bias_one, weight_two, bias_two, grad_pooled, pool_choice):
    chans, cx, cy, depth = features.shape
    nx, ny = lax.axis_size("gx"), lax.axis_size("gy")
    flags = jnp.pad(occupancy, ((1, 1), (1, 1), (0, 0))).astype(F32)
    mz = jnp.repeat(flags, 8, axis=2)
    own_f = features.transpose(1, 2, 0, 3)
    spread = np.repeat(np.eye(depth // 2, dtype=np.float32), 2, axis=1)
    both = jnp.concatenate([grad_pooled, pool_choice.astype(BF)], axis=0)
    both = jnp.dot(both, jnp.asarray(spread, BF), preferred_element_type=F32).astype(BF)
    own_p = both.transpose(1, 2, 0, 3)

    lanes = -(-(9 * chans + 1) // 128) * 128
    each = -(-3 * chans // (nx * ny))
    gin, summed = pl.pallas_call(
        functools.partial(main_kernel, nx, ny, cx, cy, depth, chans),
        out_shape=(
            jax.ShapeDtypeStruct((cx, cy, chans, depth), BF),
            jax.ShapeDtypeStruct((2, ny, nx, each, lanes), BF),
        ),
        in_specs=vmem(8),
        out_specs=tuple(vmem(2)),
        scratch_shapes=[
            pltpu.VMEM((cx + 4, cy + 4, chans, depth), BF),
            pltpu.VMEM((cx + 4, cy + 4, chans, depth), BF),
            pltpu.VMEM((cx + 4, 3 * chans, (cy + 4) * depth), BF),
            pltpu.VMEM((cx + 2, 3 * chans, (cy + 2) * depth), BF),
            pltpu.VMEM((cx + 4, 3 * chans, (cy + 4) * depth), BF),
            pltpu.VMEM((cx + 2, 3 * chans, (cy + 2) * depth), BF),
            pltpu.VMEM((2, chans, cy * depth), F32),
            pltpu.VMEM((2, 3 * chans, lanes), F32),
            pltpu.VMEM((2, ny, nx, each, lanes), BF),
            pltpu.VMEM((2, ny, nx, each, lanes), BF),
            pltpu.VMEM((2, nx, each, lanes), BF),
            pltpu.VMEM((2, nx, each, lanes), BF),
            pltpu.SemaphoreType.DMA((2, 8)),
            pltpu.SemaphoreType.DMA((2, 8)),
            pltpu.SemaphoreType.DMA((2, 2, nx)),
            pltpu.SemaphoreType.DMA((2, 2, nx)),
            pltpu.SemaphoreType.DMA((2, 2, ny)),
            pltpu.SemaphoreType.DMA((2, 2, ny)),
        ],
        compiler_params=pltpu.CompilerParams(
            collective_id=0, has_side_effects=True, vmem_limit_bytes=48 * 2**20
        ),
        name="main",
    )(
        own_f, own_p, mz,
        rows_of(weight_one), rows_of(weight_two),
        rows_of(flipped(weight_two)), rows_of(flipped(weight_one)),
        jnp.stack([bias_one, bias_two]),
    )

    total_cells = cx * nx * cy * ny * depth
    scale = 1.0 / math.sqrt(total_cells)
    sums = summed.astype(F32).reshape(2, -1, lanes)[:, : 3 * chans] * scale
    grads = sums[:, :, : 9 * chans].reshape(2, 3, chans, 3, 3, chans).transpose(0, 2, 3, 1, 4, 5)
    biases = summed[..., 9 * chans].astype(F32).reshape(2, -1)[:, :chans] * scale
    grad_input = gin.transpose(2, 0, 1, 3)
    return grad_input, grads[0], biases[0], grads[1], biases[1]


def solution(mesh):
    placed = (
        P(None, "gx", "gy", None),
        P(),
        P(),
        P(),
        P(),
        P(),
        P(None, "gx", "gy", None),
        P(None, "gx", "gy", None),
    )
    return jax.shard_map(
        body,
        mesh=mesh,
        in_specs=placed,
        out_specs=(P(None, "gx", "gy", None), P(), P(), P(), P()),
        check_vma=False,
    )
```

```python
import functools
import math

import jax
import jax.numpy as jnp
import numpy as np
from jax import lax
from jax.experimental import pallas as pl
from jax.experimental.pallas import tpu as pltpu
from jax.sharding import PartitionSpec as P

MESH = pl.DeviceIdType.MESH
HALO = 2
SIDES = ((0, -1), (0, 1), (-1, 0), (1, 0), (-1, -1), (-1, 1), (1, -1), (1, 1))
BF = jnp.bfloat16
F32 = jnp.float32


def each_row(first, end):
    def run(step):
        for row in range(first, end):
            step(row)

    return run


def edge(side, cells):
    if side == 0:
        return 0, cells
    return (0, HALO) if side < 0 else (cells - HALO, HALO)


def landing(side, cells):
    if side == 0:
        return HALO
    return HALO + cells if side < 0 else 0


def main_kernel(
    nx, ny, cx, cy, depth, chans,
    own_f, p_ref, mz_ref, w1_ref, w2_ref, w2b_ref, w1b_ref, b_ref,
    gin_ref, o_ref,
    wide_f, wide_d, s1, s2, s3, s4, bias_acc, gw_ref, g_ref, r1, h, r2,
    send_sem, recv_sem, sum_send_x, sum_recv_x, sum_send_y, sum_recv_y,
):
    gx = lax.axis_index("gx")
    gy = lax.axis_index("gy")

    def exists(sx, sy):
        ok_x = jnp.logical_and(gx + sx >= 0, gx + sx < nx)
        ok_y = jnp.logical_and(gy + sy >= 0, gy + sy < ny)
        return jnp.logical_and(ok_x, ok_y)

    def peer_x(k):
        return lax.rem(gx + k, nx)

    def peer_y(k):
        return lax.rem(gy + k, ny)

    barrier = pltpu.get_barrier_semaphore()
    for k in range(1, ny):
        pl.semaphore_signal(barrier, inc=1, device_id=(gx, peer_y(k)), device_id_type=MESH)
    for k in range(1, nx):
        pl.semaphore_signal(barrier, inc=1, device_id=(peer_x(k), gy), device_id_type=MESH)
    for sx, sy in SIDES:
        if sx and sy:
            @pl.when(exists(sx, sy))
            def _():
                pl.semaphore_signal(
                    barrier, inc=1, device_id=(gx + sx, gy + sy), device_id_type=MESH
                )
    beside_x = (gx > 0).astype(jnp.int32) + (gx < nx - 1).astype(jnp.int32)
    beside_y = (gy > 0).astype(jnp.int32) + (gy < ny - 1).astype(jnp.int32)
    pl.semaphore_wait(barrier, nx + ny - 2 + beside_x * beside_y)

    def copy_of(n, k):
        sx, sy = SIDES[k]
        fx, lx = edge(sx, cx)
        fy, ly = edge(sy, cy)
        tx, ty = landing(sx, cx), landing(sy, cy)
        if n == 0:
            out = wide_f
            src = own_f.at[fx : fx + lx, fy : fy + ly]
        else:
            out = wide_d
            fx, fy = fx + HALO, fy + HALO
            src = wide_d.at[fx : fx + lx, fy : fy + ly]
        return pltpu.make_async_remote_copy(
            src_ref=src,
            dst_ref=out.at[tx : tx + lx, ty : ty + ly],
            send_sem=send_sem.at[n, k],
            recv_sem=recv_sem.at[n, k],
            device_id=(gx + sx, gy + sy),
            device_id_type=MESH,
        )

    def send(n):
        for k, (sx, sy) in enumerate(SIDES):
            @pl.when(exists(sx, sy))
            def _():
                copy_of(n, k).start()

    def finish(n):
        for k, (sx, sy) in enumerate(SIDES):
            @pl.when(exists(sx, sy))
            def _():
                copy_of(n, k).wait_send()

            @pl.when(exists(-sx, -sy))
            def _():
                copy_of(n, k).wait_recv()

    send(0)

    same = lax.broadcasted_iota(jnp.int32, (chans, chans), 0) == lax.broadcasted_iota(
        jnp.int32, (chans, chans), 1
    )

    def column(n):
        return jnp.sum(jnp.where(same, b_ref[n : n + 1, :], 0.0), axis=1, keepdims=True)

    bias_one, bias_two = column(0), column(1)
    lane = lax.broadcasted_iota(jnp.int32, (1, depth), 1)
    not_first = lane != 0
    not_last = lane != depth - 1
    lane_odd = lane % 2

    def mask_row(x, first, count):
        brick = gx * (cx // 8) + (x + 8 - HALO) // 8
        flags = {}
        parts = []
        for y in range(first, first + count):
            by = (y + 8 - HALO) // 8
            if by not in flags:
                flags[by] = mz_ref[brick, pl.ds(gy * (cy // 8) + by, 1), :]
            parts.append(flags[by])
        return jnp.concatenate(parts, axis=1)

    def put(stack, x, value, first=0):
        count = value.shape[1] // depth
        rounded = value.astype(BF)
        wide = rounded.astype(F32)
        before, after = [], []
        for y in range(count):
            tile = wide[:, y * depth : (y + 1) * depth]
            before.append(jnp.where(not_first, pltpu.roll(tile, 1, 1), 0.0))
            after.append(jnp.where(not_last, pltpu.roll(tile, depth - 1, 1), 0.0))
        where = slice(first * depth, (first + count) * depth)
        stack[x, 0:chans, where] = jnp.concatenate(before, axis=1).astype(BF)
        stack[x, chans : 2 * chans, where] = rounded
        stack[x, 2 * chans : 3 * chans, where] = jnp.concatenate(after, axis=1).astype(BF)

    def tiles(ref, x, first, count):
        return jnp.concatenate([ref[x, y] for y in range(first, first + count)], axis=1)

    def put_cells(stack, ref, x, first, count):
        mask = mask_row(x, first, count)
        put(stack, x, jnp.where(mask > 0, tiles(ref, x, first, count).astype(F32), 0.0), first)

    def put_halo(stack, ref):
        @each_row(0, 2 * HALO)
        def _(n):
            put_cells(stack, ref, n + cx * (n // HALO), 0, cy + 2 * HALO)

        @each_row(HALO, HALO + cx)
        def _(x):
            put_cells(stack, ref, x, 0, HALO)
            put_cells(stack, ref, x, HALO + cy, HALO)

    def conv(weight, stack, x):
        width = stack.shape[2]
        rows = stack[pl.ds(x, 3)].reshape(9 * chans, width)
        full = jnp.dot(weight[...], rows, preferred_element_type=F32)
        keep = width - 2 * depth
        total = full[0:chans, 0:keep]
        total += full[chans : 2 * chans, depth : depth + keep]
        total += full[2 * chans : 3 * chans, 2 * depth : 2 * depth + keep]
        return total

    def grad(slot, delta, stack, x, first):
        width = (cy + 2) * depth
        rows = stack[pl.ds(x, 3), :, first * depth : first * depth + width].reshape(9 * chans, width)
        shifted = []
        for b in range(3):
            parts = []
            if b:
                parts.append(jnp.zeros((chans, b * depth), BF))
            parts.append(delta)
            if b < 2:
                parts.append(jnp.zeros((chans, (2 - b) * depth), BF))
            shifted.append(jnp.concatenate(parts, axis=1))
        left = jnp.concatenate(shifted, axis=0)
        gw_ref[slot, :, 0 : 9 * chans] += lax.dot_general(
            left, rows, (((1,), (1,)), ((), ())), preferred_element_type=F32
        )
        bias_acc[slot] += delta.astype(F32)

    each = g_ref.shape[3]

    def pack(slot):
        total = jnp.sum(bias_acc[slot], axis=1, keepdims=True)
        gw_ref[slot, 0:chans, 9 * chans :] = jnp.broadcast_to(
            total, (chans, gw_ref.shape[2] - 9 * chans)
        )
        for n in range(nx * ny):
            first = min(n * each, 3 * chans - each)
            g_ref[slot, n // nx, n % nx] = gw_ref[slot, first : first + each].astype(BF)

    def sum_copies(slot, phase):
        out = []
        along_y = phase in (0, 3)
        for k in range(1, ny if along_y else nx):
            peer = peer_y(k) if along_y else peer_x(k)
            if phase == 0:
                src, dst = g_ref.at[slot, peer], r1.at[slot, k]
            elif phase == 1:
                src, dst = h.at[slot, peer], r2.at[slot, k]
            elif phase == 2:
                src = dst = o_ref.at[slot, gy, gx]
            else:
                src = dst = o_ref.at[slot, gy]
            ss, rs = (sum_send_y, sum_recv_y) if along_y else (sum_send_x, sum_recv_x)
            out.append(pltpu.make_async_remote_copy(
                src_ref=src, dst_ref=dst,
                send_sem=ss.at[slot, phase // 2, k], recv_sem=rs.at[slot, phase // 2, k],
                device_id=(gx, peer) if along_y else (peer, gy), device_id_type=MESH,
            ))
        return out

    def sum_start(slot, phase):
        for copy in sum_copies(slot, phase):
            copy.start()

    def sum_finish(slot, phase):
        for copy in sum_copies(slot, phase):
            copy.wait_send()
            copy.wait_recv()
        if phase == 0:
            part = g_ref[slot, gy].astype(F32)
            for k in range(1, ny):
                part += r1[slot, k].astype(F32)
            h[slot] = part.astype(BF)
        if phase == 1:
            full = h[slot, gx].astype(F32)
            for k in range(1, nx):
                full += r2[slot, k].astype(F32)
            o_ref[slot, gy, gx] = full.astype(BF)

    gw_ref[...] = jnp.zeros_like(gw_ref)
    bias_acc[...] = jnp.zeros_like(bias_acc)

    @each_row(0, cx)
    def _(x):
        mask = mask_row(x + HALO, HALO, cy)
        put(s1, x + HALO, jnp.where(mask > 0, tiles(own_f, x, 0, cy).astype(F32), 0.0), HALO)

    finish(0)
    put_halo(s1, wide_f)

    @each_row(0, cx + 2)
    def _(x):
        mask = mask_row(x + 1, 1, cy + 2)
        pre = conv(w1_ref, s1, x) + bias_one
        put(s2, x, jnp.where(mask > 0, jnp.maximum(pre, 0.0), 0.0))

    @each_row(0, cx)
    def _(x):
        mask = mask_row(x + 2, 2, cy)
        pre = conv(w2_ref, s2, x) + bias_two
        vals, hits = [], []
        for y in range(cy):
            pooled = p_ref[x // 2, y // 2].astype(F32)
            code = (4 * (x % 2) + 2 * (y % 2) + lane_odd).astype(F32)
            vals.append(pooled[0:chans])
            hits.append(jnp.where(pooled[chans : 2 * chans] == code, 1.0, 0.0))
        up = jnp.concatenate(vals, axis=1)
        hit = jnp.concatenate(hits, axis=1) * mask
        chosen = jnp.where(pre > 0, hit, 0.0)
        delta = jnp.where(chosen > 0, up, 0.0)
        rounded = delta.astype(BF)
        for y in range(cy):
            wide_d[x + HALO, y + HALO] = rounded[:, y * depth : (y + 1) * depth]
        put(s3, x + HALO, delta, HALO)

    send(1)

    @each_row(0, cx)
    def _(x):
        delta = s3[x + HALO, chans : 2 * chans, HALO * depth : (HALO + cy) * depth]
        grad(1, delta, s2, x, 0)

    pack(1)
    finish(1)
    sum_start(1, 0)
    put_halo(s3, wide_d)

    @each_row(0, cx + 2)
    def _(x):
        back = conv(w2b_ref, s3, x)
        hidden = s2[x, chans : 2 * chans, :].astype(F32)
        put(s4, x, jnp.where(hidden > 0, back, 0.0))

    sum_finish(1, 0)
    sum_start(1, 1)

    @each_row(0, cx)
    def _(x):
        delta = s4[x + 1, chans : 2 * chans, depth : (1 + cy) * depth]
        grad(0, delta, s1, x + 1, 1)

    pack(0)
    sum_start(0, 0)
    sum_finish(1, 1)
    sum_start(1, 2)

    def last(x):
        mask = mask_row(x + 2, 2, cy)
        back = conv(w1b_ref, s4, x)
        out = jnp.where(mask > 0, back, 0.0).astype(BF)
        for y in range(cy):
            gin_ref[x, y] = out[:, y * depth : (y + 1) * depth]

    each_row(0, cx // 2)(last)
    sum_finish(0, 0)
    sum_start(0, 1)
    sum_finish(1, 2)
    sum_start(1, 3)
    each_row(cx // 2, cx)(last)
    sum_finish(0, 1)
    sum_start(0, 2)
    sum_finish(0, 2)
    sum_start(0, 3)
    sum_finish(1, 3)
    sum_finish(0, 3)


def rows_of(weight):
    channels = weight.shape[0]
    return weight.transpose(2, 0, 1, 3, 4).reshape(3 * channels, -1)


def flipped(weight):
    return jnp.flip(weight, (1, 2, 3)).transpose(4, 1, 2, 3, 0)


def vmem(count):
    return [pl.BlockSpec(memory_space=pltpu.VMEM)] * count


def body(features, occupancy, weight_one, bias_one, weight_two, bias_two, grad_pooled, pool_choice):
    chans, cx, cy, depth = features.shape
    nx, ny = lax.axis_size("gx"), lax.axis_size("gy")
    flags = jnp.pad(occupancy, ((1, 1), (1, 1), (0, 0))).astype(F32)
    mz = jnp.repeat(flags, 8, axis=2)
    own_f = features.transpose(1, 2, 0, 3)
    spread = np.repeat(np.eye(depth // 2, dtype=np.float32), 2, axis=1)
    both = jnp.concatenate([grad_pooled, pool_choice.astype(BF)], axis=0)
    both = jnp.dot(both, jnp.asarray(spread, BF), preferred_element_type=F32).astype(BF)
    own_p = both.transpose(1, 2, 0, 3)

    lanes = -(-(9 * chans + 1) // 128) * 128
    each = -(-3 * chans // (nx * ny))
    gin, summed = pl.pallas_call(
        functools.partial(main_kernel, nx, ny, cx, cy, depth, chans),
        out_shape=(
            jax.ShapeDtypeStruct((cx, cy, chans, depth), BF),
            jax.ShapeDtypeStruct((2, ny, nx, each, lanes), BF),
        ),
        in_specs=vmem(8),
        out_specs=tuple(vmem(2)),
        scratch_shapes=[
            pltpu.VMEM((cx + 4, cy + 4, chans, depth), BF),
            pltpu.VMEM((cx + 4, cy + 4, chans, depth), BF),
            pltpu.VMEM((cx + 4, 3 * chans, (cy + 4) * depth), BF),
            pltpu.VMEM((cx + 2, 3 * chans, (cy + 2) * depth), BF),
            pltpu.VMEM((cx + 4, 3 * chans, (cy + 4) * depth), BF),
            pltpu.VMEM((cx + 2, 3 * chans, (cy + 2) * depth), BF),
            pltpu.VMEM((2, chans, cy * depth), F32),
            pltpu.VMEM((2, 3 * chans, lanes), F32),
            pltpu.VMEM((2, ny, nx, each, lanes), BF),
            pltpu.VMEM((2, ny, nx, each, lanes), BF),
            pltpu.VMEM((2, nx, each, lanes), BF),
            pltpu.VMEM((2, nx, each, lanes), BF),
            pltpu.SemaphoreType.DMA((2, 8)),
            pltpu.SemaphoreType.DMA((2, 8)),
            pltpu.SemaphoreType.DMA((2, 2, nx)),
            pltpu.SemaphoreType.DMA((2, 2, nx)),
            pltpu.SemaphoreType.DMA((2, 2, ny)),
            pltpu.SemaphoreType.DMA((2, 2, ny)),
        ],
        compiler_params=pltpu.CompilerParams(
            collective_id=0, has_side_effects=True, vmem_limit_bytes=48 * 2**20
        ),
        name="main",
    )(
        own_f, own_p, mz,
        rows_of(weight_one), rows_of(weight_two),
        rows_of(flipped(weight_two)), rows_of(flipped(weight_one)),
        jnp.stack([bias_one, bias_two]),
    )

    total_cells = cx * nx * cy * ny * depth
    scale = 1.0 / math.sqrt(total_cells)
    sums = summed.astype(F32).reshape(2, -1, lanes)[:, : 3 * chans] * scale
    grads = sums[:, :, : 9 * chans].reshape(2, 3, chans, 3, 3, chans).transpose(0, 2, 3, 1, 4, 5)
    biases = summed[..., 9 * chans].astype(F32).reshape(2, -1)[:, :chans] * scale
    grad_input = gin.transpose(2, 0, 1, 3)
    return grad_input, grads[0], biases[0], grads[1], biases[1]


def solution(mesh):
    placed = (
        P(None, "gx", "gy", None),
        P(),
        P(),
        P(),
        P(),
        P(),
        P(None, "gx", "gy", None),
        P(None, "gx", "gy", None),
    )
    return jax.shard_map(
        body,
        mesh=mesh,
        in_specs=placed,
        out_specs=(P(None, "gx", "gy", None), P(), P(), P(), P()),
        check_vma=False,
    )
```
